32 devices in a mesh: row: 4 (over z), col: 8 (over y, x, core).
Axes of the slice: x: 2, y: 2, z: 4, core: 2. Of those that a mesh axis runs over, the one named last changes fastest.
Arguments:
- right_side: float32 [16, 1024, 3072], P(None, 'row', 'col'), may hold values from -100 to 100
- cond_x: float32 [1024, 3072], P('row', 'col'), may hold values from 0.25 to 4
- cond_y: float32 [1024, 3072], P('row', 'col'), may hold values from 0.25 to 4
- pad_mask: int32 [1024, 3072], P('row', 'col'), may hold values 0 or 1
Outputs:
- solution: float32 [16, 1024, 3072], P(None, 'row', 'col')
- residual: float32 [16, 1024, 3072], P(None, 'row', 'col')
The draws below stay inside these ranges and needn't reach their ends.
All inputs are finite; a program needn't handle non-finite values. No bound on the sum of `pad_mask` on one device may be relied on, other than what follows from the above.
Results may differ from the reference program's by a relative error of at most 0.0003.
Values sent between devices are 32-bit elements; how exact they have to be, the bound alone decides.
No kernel may reach another device: no remote copies, remote signals or barrier semaphores. Data moves between devices by JAX's collectives and lax.ppermute only.
A program may use at most 128 MiB of HBM per device.

```python
import math
import jax
import jax.numpy as jnp
from jax import lax

RHS = 16
ITERS = 3
NX = 1024
NY = 3072


def draw_right_side(key, part):
    key_rough = jax.random.fold_in(key, 11)
    key_scale = jax.random.fold_in(key, 12)
    row_pos = jnp.arange(NX, dtype=jnp.float32) / NX - 0.5
    col_pos = jnp.arange(NY, dtype=jnp.float32) / NY - 0.5
    pattern = jnp.exp(jax.random.uniform(key_scale, (RHS, 1, 1), jnp.float32, math.log(0.3), math.log(3.0)))
    roughness = jnp.clip(jax.random.normal(key_rough, (RHS, NX, NY), jnp.float32), -6.0, 6.0)
    growth = jnp.power(3.0, row_pos)[:, None] * jnp.power(3.0, col_pos)[None, :]
    return (pattern * growth[None] * roughness).astype(jnp.float32)


def place_ends(result, stream_key, low, high):
    longest = result.shape.index(max(result.shape))
    spots = []
    for shift in (0, 1):
        where = [jax.random.randint(jax.random.fold_in(stream_key, axis), (), 0, length) for axis, length in enumerate(result.shape)]
        where[longest] = (where[longest] + shift) % result.shape[longest]
        spots.append(tuple(where))
    return result.at[spots[0]].set(low).at[spots[1]].set(high)


def level_of(rng, extent, split, least, high):
    def one(dim, parts):
        steps = jax.random.uniform(jax.random.fold_in(jax.random.fold_in(rng, 6), dim), (parts,), jnp.float32, least / len(split), high / len(split))
        return jnp.repeat(jnp.exp(steps), extent[dim] // parts).reshape((-1,) + (1,) * (len(extent) - dim - 1))

    loudness = one(*split[0])
    for cut in split[1:]:
        loudness = loudness * one(*cut)
    return loudness


def setup_inputs(seed: int = 0) -> dict:
    key_of = jax.random.split(jax.random.key(seed), 5)
    right_side = draw_right_side(jax.random.fold_in(key_of[4], 71), 0)
    cond_x = jnp.clip(jnp.exp(math.log(4.0) - 2.7725887 * jax.random.uniform(key_of[1], (NX, NY), jnp.float32) ** level_of(key_of[1], (NX, NY), ((0, 4), (1, 8)), -0.2, 0.2)), 0.25, 4.0)
    cond_y = jnp.clip(jnp.exp(math.log(4.0) - 2.7725887 * jax.random.uniform(key_of[2], (NX, NY), jnp.float32) ** level_of(key_of[2], (NX, NY), ((0, 4), (1, 8)), -0.2, 0.2)), 0.25, 4.0)
    pad_mask = place_ends((jax.random.randint(key_of[3], (NX, NY), 0, 16) < 1).astype(jnp.int32), jax.random.fold_in(key_of[3], 1), 0, 1)
    return {"right_side": right_side, "cond_x": cond_x, "cond_y": cond_y, "pad_mask": pad_mask}


exact_precision = lax.Precision.HIGHEST

def neighbour_sum(padded, cond_x, cond_above, cond_y, cond_left):
    total = cond_x * padded[:, 2:, 1:-1] + cond_above * padded[:, :-2, 1:-1]
    return total + cond_y * padded[:, 1:-1, 2:] + cond_left * padded[:, 1:-1, :-2]

def gram(left, right):
    return jnp.einsum('kab,lab->kl', left, right, precision=exact_precision)

def combine(field, matrix):
    return jnp.einsum('kab,kl->lab', field, matrix, precision=exact_precision)

def small_solve(matrix, right):
    factor = jnp.linalg.cholesky(matrix)
    return jax.scipy.linalg.cho_solve((factor, True), right)

def reference(right_side, cond_x, cond_y, pad_mask):
    pad_nodes = pad_mask.astype(jnp.float32)
    free_nodes = 1.0 - pad_nodes
    cond_above = jnp.pad(cond_x, ((1, 0), (0, 0)))[:-1]
    cond_left = jnp.pad(cond_y, ((0, 0), (1, 0)))[:, :-1]
    diagonal = free_nodes * (cond_x + cond_above + cond_y + cond_left) + pad_nodes
    inverse = 1.0 / diagonal

    def operate(field):
        padded = jnp.pad(free_nodes * field, ((0, 0), (1, 1), (1, 1)))
        return pad_nodes * field + free_nodes * (diagonal * field - neighbour_sum(padded, cond_x, cond_above, cond_y, cond_left))
    solution = jnp.zeros_like(right_side)
    residual = right_side
    precond = residual * inverse
    direction = precond
    gram_now = gram(residual, precond)
    for iteration in range(ITERS):
        image = operate(direction)
        alpha_block = small_solve(gram(direction, image), gram_now)
        solution = solution + combine(direction, alpha_block)
        residual = residual - combine(image, alpha_block)
        precond = residual * inverse
        gram_next = gram(residual, precond)
        beta_block = small_solve(gram_now, gram_next)
        direction = precond + combine(direction, beta_block)
        gram_now = gram_next
    return (solution, residual)
```

```python
import functools

import jax
import jax.numpy as jnp
from jax import lax
from jax.experimental import pallas as pl
from jax.experimental.pallas import tpu as pltpu
from jax.sharding import PartitionSpec as P

ITERS = 3
DEPTH = ITERS + 1
SUB = 8
LANE = 128
MOMENTS = 2 * ITERS

exact = lax.Precision.HIGHEST


def split(x):
    high = x.astype(jnp.bfloat16)
    low = (x - high.astype(jnp.float32)).astype(jnp.bfloat16)
    return high, low


def rows_of(ref, k, start):
    return ref[k, pl.ds(pl.multiple_of(start, SUB), SUB), :]


def plane_rows(ref, start):
    return ref[pl.ds(pl.multiple_of(start, SUB), SUB), :]


def stencil(ref, k, slab, last, coefs, row):
    above = rows_of(ref, k, jnp.maximum(slab - 1, 0) * SUB)
    here = rows_of(ref, k, slab * SUB)
    below = rows_of(ref, k, jnp.minimum(slab + 1, last) * SUB)
    down = pltpu.roll(jnp.where(row == 0, below, here), SUB - 1, 0)
    up = pltpu.roll(jnp.where(row == SUB - 1, above, here), 1, 0)
    wide = here.shape[1]
    right = pltpu.roll(here, wide - 1, 1)
    left = pltpu.roll(here, 1, 1)
    to_down, to_up, to_right, to_left = coefs
    return here, (to_down * down + to_up * up) + (to_right * right + to_left * left)


def nt_dot(a, b):
    return lax.dot_general(a, b, (((1,), (1,)), ((), ())), preferred_element_type=jnp.float32)


def tn_dot(a, b):
    return lax.dot_general(a, b, (((0,), (0,)), ((), ())), precision=exact, preferred_element_type=jnp.float32)


def hi_dot(a, b):
    return jnp.dot(a, b, precision=exact, preferred_element_type=jnp.float32)


def spread(fields):
    big = fields * SUB
    r = lax.broadcasted_iota(jnp.int32, (big, fields), 0) // SUB
    c = lax.broadcasted_iota(jnp.int32, (big, fields), 1)
    return (r == c).astype(jnp.float32)


def same_row(big):
    r = lax.broadcasted_iota(jnp.int32, (big, big), 0) % SUB
    c = lax.broadcasted_iota(jnp.int32, (big, big), 1) % SUB
    return r == c


def basis_kernel(r_ref, top_ref, bottom_ref, side_ref, dinv_ref, dn_ref, up_ref, rt_ref, lf_ref,
                 m_ref, x0_ref, x1_ref, x2_ref, acc_ref):
    fields, rows, cols = r_ref.shape
    slabs = rows // SUB
    last = slabs + 1
    big = fields * SUB
    wide = dinv_ref.shape[1]
    row = lax.broadcasted_iota(jnp.int32, (SUB, wide), 0)

    for k in range(fields):
        x0_ref[k, 0:SUB, :] = top_ref[k] * dinv_ref[0:SUB, :]
        x0_ref[k, rows + SUB:rows + 2 * SUB, :] = bottom_ref[k] * dinv_ref[rows + SUB:rows + 2 * SUB, :]

    @pl.loop(0, slabs)
    def _(i):
        scale = plane_rows(dinv_ref, (i + 1) * SUB)
        for k in range(fields):
            x0_ref[k, pl.ds(pl.multiple_of((i + 1) * SUB, SUB), SUB), 0:cols] = rows_of(r_ref, k, i * SUB) * scale[:, :cols]
            x0_ref[k, pl.ds(pl.multiple_of((i + 1) * SUB, SUB), SUB), cols:wide] = rows_of(side_ref, k, i * SUB) * scale[:, cols:]

    acc_ref[...] = jnp.zeros_like(acc_ref)

    def sweep(src, dst, i):
        at = pl.multiple_of(i * SUB, SUB)
        coefs = [plane_rows(ref, i * SUB) for ref in (dn_ref, up_ref, rt_ref, lf_ref)]
        olds, news = [], []
        for k in range(fields):
            here, new = stencil(src, k, i, last, coefs, row)
            if dst is not None:
                dst[k, pl.ds(at, SUB), :] = new
            olds.append(here[:, :cols])
            news.append(new[:, :cols])
        return olds, news

    for t, (src, dst) in enumerate(((x0_ref, x1_ref), (x1_ref, x2_ref), (x2_ref, None))):
        if dst is not None:
            sweep(src, dst, 0)
            sweep(src, dst, last)

        @pl.loop(1, last)
        def _(i, src=src, dst=dst, t=t):
            olds, news = sweep(src, dst, i)
            old_hi, old_lo = split(jnp.concatenate(olds, 0))
            new_hi, new_lo = split(jnp.concatenate(news, 0))
            acc_ref[t, 0] += nt_dot(old_hi, old_hi)
            acc_ref[t, 1] += nt_dot(old_hi, old_lo)
            acc_ref[t, 2] += nt_dot(old_hi, new_hi) + nt_dot(old_hi, new_lo) + nt_dot(old_lo, new_hi)

    gather = spread(fields)
    keep = same_row(big)
    for t in range(ITERS):
        cross = acc_ref[t, 1]
        even = hi_dot(jnp.where(keep, acc_ref[t, 0], 0.0), gather)
        m_ref[2 * t] = tn_dot(gather, even)
        crossed = tn_dot(gather, hi_dot(jnp.where(keep, cross, 0.0), gather))
        m_ref[2 * t] += crossed + crossed.T
        odd = hi_dot(jnp.where(keep, acc_ref[t, 2], 0.0), gather)
        m_ref[2 * t + 1] = tn_dot(gather, odd)


def small_solve(a, b):
    n = a.shape[0]
    row = lax.broadcasted_iota(jnp.int32, a.shape, 0)
    for p in range(n):
        inv = 1.0 / a[p:p + 1, p:p + 1]
        pa = a[p:p + 1, :] * inv
        pb = b[p:p + 1, :] * inv
        col = a[:, p:p + 1]
        a = jnp.where(row == p, pa, a - col * pa)
        b = jnp.where(row == p, pb, b - col * pb)
    return b


def coefficients(m, hankel_ref):
    n = m[0].shape[0]
    deg = ITERS + 1
    hankel_ref[...] = jnp.zeros_like(hankel_ref)
    for i in range(deg):
        for j in range(deg):
            if i + j < MOMENTS:
                hankel_ref[i * n:(i + 1) * n, j * n:(j + 1) * n] = m[i + j]
    hankel = hankel_ref[...]
    zero = jnp.zeros((n, n), jnp.float32)
    r = lax.broadcasted_iota(jnp.int32, (n, n), 0)
    c = lax.broadcasted_iota(jnp.int32, (n, n), 1)
    eye = (r == c).astype(jnp.float32)
    precond = jnp.concatenate([eye] + [zero] * (deg - 1), 0)
    direction = precond
    total = jnp.zeros_like(precond)
    gram_now = m[0]
    for it in range(ITERS):
        image = direction - jnp.concatenate([zero, direction[:-n]], 0)
        curvature = tn_dot(direction, hi_dot(hankel, image))
        alpha = small_solve(curvature, gram_now)
        total = total + hi_dot(direction, alpha)
        if it + 1 < ITERS:
            precond = precond - hi_dot(image, alpha)
            gram_next = tn_dot(precond, hi_dot(hankel, precond))
            beta = small_solve(gram_now, gram_next)
            direction = precond + hi_dot(direction, beta)
            gram_now = gram_next
    return total


def combine_kernel(m_ref, x0_ref, x1_ref, x2_ref, dinv_ref, dsq_ref, dn_ref, up_ref, rt_ref, lf_ref,
                   s_ref, res_ref, y_ref, hankel_ref, whi_ref, wlo_ref):
    fields, block, cols = s_ref.shape
    rows = x0_ref.shape[1] - 2 * SUB
    wide = x0_ref.shape[2]
    last = rows // SUB + 1
    big = fields * SUB
    g = pl.program_id(0)
    per = block // SUB
    row = lax.broadcasted_iota(jnp.int32, (SUB, wide), 0)

    @pl.when(g == 0)
    def _():
        total = coefficients([m_ref[j] for j in range(MOMENTS)], hankel_ref)
        out = spread(fields)
        keep = same_row(big)
        for j in range(ITERS):
            block_t = total[j * fields:(j + 1) * fields].T
            wide_t = lax.dot_general(hi_dot(out, block_t), out, (((1,), (1,)), ((), ())),
                                     precision=exact, preferred_element_type=jnp.float32)
            hi, lo = split(jnp.where(keep, wide_t, 0.0))
            whi_ref[:, j * big:(j + 1) * big] = hi
            wlo_ref[:, j * big:(j + 1) * big] = lo

    @pl.loop(jnp.where(g == 0, 0, g * per + 2), g * per + per + 2)
    def _(i):
        at = pl.multiple_of(i * SUB, SUB)
        stacked = jnp.concatenate([ref[k, pl.ds(at, SUB), :] for ref in (x0_ref, x1_ref, x2_ref) for k in range(fields)], 0)
        hi, lo = split(stacked)
        whi = whi_ref[...]
        y = (jnp.dot(whi, hi, preferred_element_type=jnp.float32)
             + jnp.dot(wlo_ref[...], hi, preferred_element_type=jnp.float32)
             + jnp.dot(whi, lo, preferred_element_type=jnp.float32))
        for k in range(fields):
            y_ref[k, pl.ds(at, SUB), :] = y[k * SUB:(k + 1) * SUB]

    @pl.loop(0, per)
    def _(q):
        i = g * per + q + 1
        at = pl.multiple_of(i * SUB, SUB)
        to = pl.multiple_of(q * SUB, SUB)
        coefs = [plane_rows(ref, i * SUB) for ref in (dn_ref, up_ref, rt_ref, lf_ref)]
        inv = plane_rows(dinv_ref, i * SUB)[:, :cols]
        root = plane_rows(dsq_ref, i * SUB)[:, :cols]
        for k in range(fields):
            here, swept = stencil(y_ref, k, i, last, coefs, row)
            here = here[:, :cols]
            s_ref[k, pl.ds(to, SUB), :] = here * inv
            res_ref[k, pl.ds(to, SUB), :] = root * (x0_ref[k, pl.ds(at, SUB), :][:, :cols] - here + swept[:, :cols])


def halo(cells, axis, dim):
    count = lax.axis_size(axis)
    size = cells.shape[dim]
    head = lax.slice_in_dim(cells, 0, DEPTH, axis=dim)
    tail = lax.slice_in_dim(cells, size - DEPTH, size, axis=dim)
    before = lax.ppermute(tail, axis, [(i, i + 1) for i in range(count - 1)])
    after = lax.ppermute(head, axis, [(i + 1, i) for i in range(count - 1)])
    return before, after


def shards(right_side, cond_x, cond_y, pad_mask):
    fields, rows, cols = right_side.shape
    wide = cols + LANE
    free = 1.0 - pad_mask.astype(jnp.float32)
    planes = jnp.stack([cond_x, cond_y, free])
    row_strip = jnp.concatenate([right_side[:, :DEPTH], right_side[:, rows - DEPTH:]], 1)
    row_strip = jnp.concatenate([row_strip, jnp.concatenate([planes[:, :DEPTH], planes[:, rows - DEPTH:]], 1)], 0)
    above, below = halo(row_strip, "row", 1)
    ends = [slice(0, DEPTH), slice(cols - DEPTH, cols)]

    def column_strip(e):
        mid = jnp.concatenate([right_side[:, :, e], planes[:, :, e]], 0)
        full = jnp.concatenate([above[:, :, e], mid, below[:, :, e]], 1)
        return jnp.swapaxes(full, 1, 2)

    strip = jnp.concatenate([column_strip(e) for e in ends], 1)
    left, right = halo(strip, "col", 1)
    gap = jnp.zeros((left.shape[0], LANE - 2 * DEPTH, left.shape[2]), jnp.float32)
    side = jnp.swapaxes(jnp.concatenate([right, gap, left], 1), 1, 2)
    edge = SUB - DEPTH
    top = jnp.pad(jnp.concatenate([above, side[:, :DEPTH]], 2), ((0, 0), (edge, 0), (0, 0)))
    bottom = jnp.pad(jnp.concatenate([below, side[:, DEPTH + rows:]], 2), ((0, 0), (0, edge), (0, 0)))
    side = side[:, DEPTH:DEPTH + rows]
    ext = jnp.concatenate([top[fields:], jnp.concatenate([planes, side[fields:]], 2), bottom[fields:]], 1)
    cx, cy, fr = ext[0], ext[1], ext[2]
    diagonal = fr * (cx + jnp.roll(cx, 1, 0) + cy + jnp.roll(cy, 1, 1)) + (1.0 - fr)
    root = jnp.sqrt(diagonal)
    dinv = 1.0 / root
    scale = fr * dinv
    to_down = cx * scale * jnp.roll(scale, -1, 0)
    to_up = jnp.roll(to_down, 1, 0)
    to_right = cy * scale * jnp.roll(scale, -1, 1)
    to_left = jnp.roll(to_right, 1, 1)

    ext_shape = (fields, rows + 2 * SUB, wide)
    big = fields * SUB
    field_out = FIELD(ext_shape)
    vmem = pl.BlockSpec(memory_space=pltpu.VMEM)
    m, x0, x1, x2 = pl.pallas_call(
        basis_kernel,
        out_shape=[jax.ShapeDtypeStruct((MOMENTS, fields, fields), jnp.float32)] + [field_out] * 3,
        in_specs=[vmem] * 9,
        out_specs=[vmem] * 4,
        scratch_shapes=[pltpu.VMEM((ITERS, 3, big, big), jnp.float32)],
        name="basis",
        compiler_params=pltpu.CompilerParams(vmem_limit_bytes=BASIS_LIMIT),
    )(right_side, top[:fields], bottom[:fields], side[:fields], dinv, to_down, to_up, to_right, to_left)
    m = lax.psum(m, ("row", "col"))
    block = 4 * SUB
    while rows % block:
        block //= 2
    whole = lambda shape: pl.BlockSpec(shape, lambda g: (0,) * len(shape))
    plane = whole((rows + 2 * SUB, wide))
    out_spec = pl.BlockSpec((fields, block, cols), lambda g: (0, g, 0))
    return tuple(pl.pallas_call(
        combine_kernel,
        grid=(rows // block,),
        out_shape=[jax.ShapeDtypeStruct(right_side.shape, jnp.float32)] * 2,
        in_specs=[vmem] * 10,
        out_specs=[out_spec] * 2,
        scratch_shapes=[
            pltpu.VMEM(ext_shape, jnp.float32),
            pltpu.VMEM(((ITERS + 1) * fields,) * 2, jnp.float32),
            pltpu.VMEM((big, ITERS * big), jnp.bfloat16),
            pltpu.VMEM((big, ITERS * big), jnp.bfloat16),
        ],
        name="combine",
        compiler_params=pltpu.CompilerParams(vmem_limit_bytes=COMBINE_LIMIT, dimension_semantics=("arbitrary",)),
    )(m, x0, x1, x2, dinv, root, to_down, to_up, to_right, to_left))


FIELD = lambda shape: jax.ShapeDtypeStruct(shape, jnp.float32)
BASIS_LIMIT = 60 * 2**20
COMBINE_LIMIT = 60 * 2**20


def solution(mesh):
    in_specs = (P(None, "row", "col"), P("row", "col"), P("row", "col"), P("row", "col"))
    out_specs = (P(None, "row", "col"), P(None, "row", "col"))
    return jax.shard_map(shards, mesh=mesh, in_specs=in_specs, out_specs=out_specs, check_vma=False)
```

```python
import functools

import jax
import jax.numpy as jnp
from jax import lax
from jax.experimental import pallas as pl
from jax.experimental.pallas import tpu as pltpu
from jax.sharding import PartitionSpec as P

ITERS = 3
DEPTH = ITERS + 1
SUB = 8
LANE = 128
MOMENTS = 2 * ITERS

exact = lax.Precision.HIGHEST


def split(x):
    high = x.astype(jnp.bfloat16)
    low = (x - high.astype(jnp.float32)).astype(jnp.bfloat16)
    return high, low


def rows_of(ref, k, start):
    return ref[k, pl.ds(pl.multiple_of(start, SUB), SUB), :]


def plane_rows(ref, start):
    return ref[pl.ds(pl.multiple_of(start, SUB), SUB), :]


def stencil(ref, k, slab, last, coefs, row):
    above = rows_of(ref, k, jnp.maximum(slab - 1, 0) * SUB)
    here = rows_of(ref, k, slab * SUB)
    below = rows_of(ref, k, jnp.minimum(slab + 1, last) * SUB)
    down = pltpu.roll(jnp.where(row == 0, below, here), SUB - 1, 0)
    up = pltpu.roll(jnp.where(row == SUB - 1, above, here), 1, 0)
    wide = here.shape[1]
    right = pltpu.roll(here, wide - 1, 1)
    left = pltpu.roll(here, 1, 1)
    to_down, to_up, to_right, to_left = coefs
    return here, (to_down * down + to_up * up) + (to_right * right + to_left * left)


def nt_dot(a, b):
    return lax.dot_general(a, b, (((1,), (1,)), ((), ())), preferred_element_type=jnp.float32)


def tn_dot(a, b):
    return lax.dot_general(a, b, (((0,), (0,)), ((), ())), precision=exact, preferred_element_type=jnp.float32)


def hi_dot(a, b):
    return jnp.dot(a, b, precision=exact, preferred_element_type=jnp.float32)


def spread(fields):
    big = fields * SUB
    r = lax.broadcasted_iota(jnp.int32, (big, fields), 0) // SUB
    c = lax.broadcasted_iota(jnp.int32, (big, fields), 1)
    return (r == c).astype(jnp.float32)


def same_row(big):
    r = lax.broadcasted_iota(jnp.int32, (big, big), 0) % SUB
    c = lax.broadcasted_iota(jnp.int32, (big, big), 1) % SUB
    return r == c


def basis_kernel(r_ref, top_ref, bottom_ref, side_ref, dinv_ref, dn_ref, up_ref, rt_ref, lf_ref,
                 m_ref, x0_out, x1_out, x2_out, x0_ref, x1_ref, x2_ref, acc_ref, sems):
    fields, rows, cols = r_ref.shape
    slabs = rows // SUB
    last = slabs + 1
    big = fields * SUB
    wide = dinv_ref.shape[1]
    row = lax.broadcasted_iota(jnp.int32, (SUB, wide), 0)

    for k in range(fields):
        x0_ref[k, 0:SUB, :] = top_ref[k] * dinv_ref[0:SUB, :]
        x0_ref[k, rows + SUB:rows + 2 * SUB, :] = bottom_ref[k] * dinv_ref[rows + SUB:rows + 2 * SUB, :]

    @pl.loop(0, slabs)
    def _(i):
        scale = plane_rows(dinv_ref, (i + 1) * SUB)
        for k in range(fields):
            x0_ref[k, pl.ds(pl.multiple_of((i + 1) * SUB, SUB), SUB), 0:cols] = rows_of(r_ref, k, i * SUB) * scale[:, :cols]
            x0_ref[k, pl.ds(pl.multiple_of((i + 1) * SUB, SUB), SUB), cols:wide] = rows_of(side_ref, k, i * SUB) * scale[:, cols:]

    acc_ref[...] = jnp.zeros_like(acc_ref)
    copies = [pltpu.make_async_copy(a, b, sems.at[j]) for j, (a, b) in
              enumerate(((x0_ref, x0_out), (x1_ref, x1_out), (x2_ref, x2_out)))]

    def sweep(src, dst, i):
        at = pl.multiple_of(i * SUB, SUB)
        coefs = [plane_rows(ref, i * SUB) for ref in (dn_ref, up_ref, rt_ref, lf_ref)]
        olds, news = [], []
        for k in range(fields):
            here, new = stencil(src, k, i, last, coefs, row)
            if dst is not None:
                dst[k, pl.ds(at, SUB), :] = new
            olds.append(here[:, :cols])
            news.append(new[:, :cols])
        return olds, news

    for t, (src, dst) in enumerate(((x0_ref, x1_ref), (x1_ref, x2_ref), (x2_ref, None))):
        copies[t].start()
        if dst is not None:
            sweep(src, dst, 0)
            sweep(src, dst, last)

        @pl.loop(1, last)
        def _(i, src=src, dst=dst, t=t):
            olds, news = sweep(src, dst, i)
            old_hi, old_lo = split(jnp.concatenate(olds, 0))
            new_hi, new_lo = split(jnp.concatenate(news, 0))
            acc_ref[t, 0] += nt_dot(old_hi, old_hi)
            acc_ref[t, 1] += nt_dot(old_hi, old_lo)
            acc_ref[t, 2] += nt_dot(old_hi, new_hi) + nt_dot(old_hi, new_lo) + nt_dot(old_lo, new_hi)

    gather = spread(fields)
    keep = same_row(big)
    for t in range(ITERS):
        cross = acc_ref[t, 1]
        even = hi_dot(jnp.where(keep, acc_ref[t, 0], 0.0), gather)
        m_ref[2 * t] = tn_dot(gather, even)
        crossed = tn_dot(gather, hi_dot(jnp.where(keep, cross, 0.0), gather))
        m_ref[2 * t] += crossed + crossed.T
        odd = hi_dot(jnp.where(keep, acc_ref[t, 2], 0.0), gather)
        m_ref[2 * t + 1] = tn_dot(gather, odd)
    for copy in copies:
        copy.wait()


def small_solve(a, b):
    n = a.shape[0]
    row = lax.broadcasted_iota(jnp.int32, a.shape, 0)
    for p in range(n):
        inv = 1.0 / a[p:p + 1, p:p + 1]
        pa = a[p:p + 1, :] * inv
        pb = b[p:p + 1, :] * inv
        col = a[:, p:p + 1]
        a = jnp.where(row == p, pa, a - col * pa)
        b = jnp.where(row == p, pb, b - col * pb)
    return b


def coefficients(m, hankel_ref):
    n = m[0].shape[0]
    deg = ITERS + 1
    hankel_ref[...] = jnp.zeros_like(hankel_ref)
    for i in range(deg):
        for j in range(deg):
            if i + j < MOMENTS:
                hankel_ref[i * n:(i + 1) * n, j * n:(j + 1) * n] = m[i + j]
    hankel = hankel_ref[...]
    zero = jnp.zeros((n, n), jnp.float32)
    r = lax.broadcasted_iota(jnp.int32, (n, n), 0)
    c = lax.broadcasted_iota(jnp.int32, (n, n), 1)
    eye = (r == c).astype(jnp.float32)
    precond = jnp.concatenate([eye] + [zero] * (deg - 1), 0)
    direction = precond
    total = jnp.zeros_like(precond)
    gram_now = m[0]
    for it in range(ITERS):
        image = direction - jnp.concatenate([zero, direction[:-n]], 0)
        curvature = tn_dot(direction, hi_dot(hankel, image))
        alpha = small_solve(curvature, gram_now)
        total = total + hi_dot(direction, alpha)
        if it + 1 < ITERS:
            precond = precond - hi_dot(image, alpha)
            gram_next = tn_dot(precond, hi_dot(hankel, precond))
            beta = small_solve(gram_now, gram_next)
            direction = precond + hi_dot(direction, beta)
            gram_now = gram_next
    return total


def combine_kernel(m_ref, x0_ref, x1_ref, x2_ref, dinv_ref, dsq_ref, dn_ref, up_ref, rt_ref, lf_ref,
                   s_ref, res_ref, y_ref, diff_ref, hankel_ref, whi_ref, wlo_ref):
    fields, block, cols = s_ref.shape
    wide = x0_ref.shape[2]
    last = y_ref.shape[1] // SUB - 1
    big = fields * SUB
    g = pl.program_id(0)
    per = block // SUB
    row = lax.broadcasted_iota(jnp.int32, (SUB, wide), 0)

    @pl.when(g == 0)
    def _():
        total = coefficients([m_ref[j] for j in range(MOMENTS)], hankel_ref)
        out = spread(fields)
        keep = same_row(big)
        for j in range(ITERS):
            block_t = total[j * fields:(j + 1) * fields].T
            wide_t = lax.dot_general(hi_dot(out, block_t), out, (((1,), (1,)), ((), ())),
                                     precision=exact, preferred_element_type=jnp.float32)
            hi, lo = split(jnp.where(keep, wide_t, 0.0))
            whi_ref[:, j * big:(j + 1) * big] = hi
            wlo_ref[:, j * big:(j + 1) * big] = lo

    @pl.loop(0, per)
    def _(q):
        frm = pl.multiple_of(q * SUB, SUB)
        at = pl.multiple_of((g * per + q) * SUB, SUB)
        stacked = jnp.concatenate([ref[k, pl.ds(frm, SUB), :] for ref in (x0_ref, x1_ref, x2_ref) for k in range(fields)], 0)
        hi, lo = split(stacked)
        whi = whi_ref[...]
        y = (jnp.dot(whi, hi, preferred_element_type=jnp.float32)
             + jnp.dot(wlo_ref[...], hi, preferred_element_type=jnp.float32)
             + jnp.dot(whi, lo, preferred_element_type=jnp.float32))
        for k in range(fields):
            y_k = y[k * SUB:(k + 1) * SUB]
            y_ref[k, pl.ds(at, SUB), :] = y_k
            diff_ref[k, pl.ds(at, SUB), :] = stacked[k * SUB:(k + 1) * SUB, :cols] - y_k[:, :cols]

    @pl.when(g > 0)
    def _():
        @pl.loop(0, per)
        def _(q):
            i = (g - 1) * per + q + 1
            at = pl.multiple_of(i * SUB, SUB)
            to = pl.multiple_of(q * SUB, SUB)
            coefs = [plane_rows(ref, i * SUB) for ref in (dn_ref, up_ref, rt_ref, lf_ref)]
            inv = plane_rows(dinv_ref, i * SUB)[:, :cols]
            root = plane_rows(dsq_ref, i * SUB)[:, :cols]
            for k in range(fields):
                here, swept = stencil(y_ref, k, i, last, coefs, row)
                s_ref[k, pl.ds(to, SUB), :] = here[:, :cols] * inv
                res_ref[k, pl.ds(to, SUB), :] = root * (diff_ref[k, pl.ds(at, SUB), :] + swept[:, :cols])


def halo(cells, axis, dim):
    count = lax.axis_size(axis)
    size = cells.shape[dim]
    head = lax.slice_in_dim(cells, 0, DEPTH, axis=dim)
    tail = lax.slice_in_dim(cells, size - DEPTH, size, axis=dim)
    before = lax.ppermute(tail, axis, [(i, i + 1) for i in range(count - 1)])
    after = lax.ppermute(head, axis, [(i + 1, i) for i in range(count - 1)])
    return before, after


def summed(x, axes):
    for axis in axes:
        n = lax.axis_size(axis)
        if n & (n - 1):
            x = lax.psum(x, axis)
            continue
        step = 1
        while step < n:
            far = (n // step).bit_length() % 2 == 1
            got = [lax.ppermute(x, axis, [(i, i ^ (step * o)) for i in range(n)]) for o in ((1, 2, 3) if far else (1,))]
            x = x + got[0]
            if far:
                x = x + (got[1] + got[2])
            step *= 4 if far else 2
    return x


def shards(right_side, cond_x, cond_y, pad_mask):
    fields, rows, cols = right_side.shape
    wide = cols + LANE
    free = 1.0 - pad_mask.astype(jnp.float32)
    planes = jnp.stack([cond_x, cond_y, free])
    row_strip = jnp.concatenate([right_side[:, :DEPTH], right_side[:, rows - DEPTH:]], 1)
    row_strip = jnp.concatenate([row_strip, jnp.concatenate([planes[:, :DEPTH], planes[:, rows - DEPTH:]], 1)], 0)
    above, below = halo(row_strip, "row", 1)
    ends = [slice(0, DEPTH), slice(cols - DEPTH, cols)]

    def column_strip(e):
        mid = jnp.concatenate([right_side[:, :, e], planes[:, :, e]], 0)
        full = jnp.concatenate([above[:, :, e], mid, below[:, :, e]], 1)
        return jnp.swapaxes(full, 1, 2)

    strip = jnp.concatenate([column_strip(e) for e in ends], 1)
    left, right = halo(strip, "col", 1)
    gap = jnp.zeros((left.shape[0], LANE - 2 * DEPTH, left.shape[2]), jnp.float32)
    side = jnp.swapaxes(jnp.concatenate([right, gap, left], 1), 1, 2)
    edge = SUB - DEPTH
    top = jnp.pad(jnp.concatenate([above, side[:, :DEPTH]], 2), ((0, 0), (edge, 0), (0, 0)))
    bottom = jnp.pad(jnp.concatenate([below, side[:, DEPTH + rows:]], 2), ((0, 0), (0, edge), (0, 0)))
    side = side[:, DEPTH:DEPTH + rows]
    ext = jnp.concatenate([top[fields:], jnp.concatenate([planes, side[fields:]], 2), bottom[fields:]], 1)
    cx, cy, fr = ext[0], ext[1], ext[2]
    diagonal = fr * (cx + jnp.roll(cx, 1, 0) + cy + jnp.roll(cy, 1, 1)) + (1.0 - fr)
    root = jnp.sqrt(diagonal)
    dinv = 1.0 / root
    scale = fr * dinv
    to_down = cx * scale * jnp.roll(scale, -1, 0)
    to_up = jnp.roll(to_down, 1, 0)
    to_right = cy * scale * jnp.roll(scale, -1, 1)
    to_left = jnp.roll(to_right, 1, 1)

    ext_shape = (fields, rows + 2 * SUB, wide)
    big = fields * SUB
    field_out = jax.ShapeDtypeStruct(ext_shape, jnp.float32)
    vmem = pl.BlockSpec(memory_space=pltpu.VMEM)
    m, x0, x1, x2 = pl.pallas_call(
        basis_kernel,
        out_shape=[jax.ShapeDtypeStruct((MOMENTS, fields, fields), jnp.float32)] + [field_out] * 3,
        in_specs=[vmem] * 9,
        out_specs=[vmem] + [pl.BlockSpec(memory_space=pl.ANY)] * 3,
        scratch_shapes=[pltpu.VMEM(ext_shape, jnp.float32)] * 3 + [pltpu.VMEM((ITERS, 3, big, big), jnp.float32), pltpu.SemaphoreType.DMA((3,))],
        name="basis",
        compiler_params=pltpu.CompilerParams(vmem_limit_bytes=BASIS_LIMIT),
    )(right_side, top[:fields], bottom[:fields], side[:fields], dinv, to_down, to_up, to_right, to_left)
    m = summed(m.reshape(-1, LANE), ("col", "row")).reshape(m.shape)
    block = 2 * SUB
    assert rows % block == 0 and cols % LANE == 0
    x_spec = pl.BlockSpec((fields, block, wide), lambda g: (0, g, 0))
    out_spec = pl.BlockSpec((fields, block, cols), lambda g: (0, jnp.maximum(g - 1, 0), 0))
    return tuple(pl.pallas_call(
        combine_kernel,
        grid=(rows // block + 1,),
        out_shape=[jax.ShapeDtypeStruct(right_side.shape, jnp.float32)] * 2,
        in_specs=[vmem] + [x_spec] * 3 + [vmem] * 6,
        out_specs=[out_spec] * 2,
        scratch_shapes=[
            pltpu.VMEM(ext_shape, jnp.float32),
            pltpu.VMEM((fields, rows + 2 * SUB, cols), jnp.float32),
            pltpu.VMEM(((ITERS + 1) * fields,) * 2, jnp.float32),
            pltpu.VMEM((big, ITERS * big), jnp.bfloat16),
            pltpu.VMEM((big, ITERS * big), jnp.bfloat16),
        ],
        name="combine",
        compiler_params=pltpu.CompilerParams(vmem_limit_bytes=COMBINE_LIMIT, dimension_semantics=("arbitrary",)),
    )(m, x0, x1, x2, dinv, root, to_down, to_up, to_right, to_left))


BASIS_LIMIT = 60 * 2**20
COMBINE_LIMIT = 60 * 2**20


def solution(mesh):
    in_specs = (P(None, "row", "col"), P("row", "col"), P("row", "col"), P("row", "col"))
    out_specs = (P(None, "row", "col"), P(None, "row", "col"))
    return jax.shard_map(shards, mesh=mesh, in_specs=in_specs, out_specs=out_specs, check_vma=False)
```
